32 devices in a mesh: rows: 4 (over z), cols: 8 (over y, x, core).
Axes of the slice: x: 2, y: 2, z: 4, core: 2. Of those that a mesh axis runs over, the one named last changes fastest.
Arguments:
- genotypes: bfloat16 [30720, 2048], P(('rows', 'cols')), may hold values from 0 to 2
- probes: bfloat16 [30720, 128], P(('rows', 'cols')), may hold values from -6 to 6
- missing_codes: int32 [30720], P(('rows', 'cols')), may hold values from 0 to 31
Outputs:
- basis: bfloat16 [30720, 128], P(('rows', 'cols'))
- scores: bfloat16 [2048, 128], replicated
The draws below stay inside these ranges and needn't reach their ends.
Inputs may be any that keep to these rules, and one draw needn't show every extreme that they name: `missing_codes`: A code c below 16 marks SNPs c * 128 to (c + 1) * 128 - 1 as missing for that individual; larger codes mark none.
All inputs are finite; a program needn't handle non-finite values.
Results may differ from the reference program's by a relative error of at most 0.017.
Values sent between devices are 32-bit elements; how exact they have to be, the bound alone decides.
A program may use at most 64 MiB of HBM per device.

```python
import math
import jax
import jax.numpy as jnp
from jax import lax

M = 2048
B = 128
BLOCK_SNPS = 128
NBLK = 16
NTOT = 30720
N_ROWS = 4


def draw_genotypes(key, part):
    key_freq, key_noise = jax.random.split(jax.random.fold_in(key, 17))
    lowest = 0.002
    freq = jnp.exp(jax.random.uniform(key_freq, (M,), jnp.float32, jnp.log(lowest), jnp.log(0.5)))
    ramp = 0.5 + jnp.arange(NTOT, dtype=jnp.float32) / NTOT
    effective = jnp.minimum(freq[None, :] * ramp[:, None], 0.75)
    spread = jnp.sqrt(2.0 * effective * (1.0 - effective))
    noise = jnp.clip(jax.random.normal(key_noise, (NTOT, M), jnp.float32), -3.0, 3.0)
    return jnp.clip(2.0 * effective + spread * noise, 0.0, 2.0).astype(jnp.bfloat16)


def with_ends(values, own_key, least, top_value):
    longest = values.shape.index(max(values.shape))
    spots = []
    for shift in (0, 1):
        where = [jax.random.randint(jax.random.fold_in(own_key, axis), (), 0, length) for axis, length in enumerate(values.shape)]
        where[longest] = (where[longest] + shift) % values.shape[longest]
        spots.append(tuple(where))
    return values.at[spots[0]].set(least).at[spots[1]].set(top_value)


def shard_levels(key, shape, cuts, smallest, top_value):
    loudness = 1.0
    for position, blocks in cuts:
        draws = jax.random.uniform(jax.random.fold_in(jax.random.fold_in(key, 6), position), (blocks,), jnp.float32, smallest / len(cuts), top_value / len(cuts))
        loudness = loudness * jnp.repeat(jnp.exp(draws), shape[position] // blocks).reshape((-1,) + (1,) * (len(shape) - 1 - position))
    return loudness


def gaussian(key, extent, scale, bound, cuts=(), kind=jnp.bfloat16):
    entries = scale * jax.random.normal(key, extent, jnp.float32)
    if cuts:
        entries = entries * shard_levels(key, extent, cuts, -0.22, 0.18)
    return jnp.clip(entries, -bound, bound).astype(kind)


def setup_inputs(seed: int = 0) -> dict:
    key_of = jax.random.split(jax.random.key(seed), 4)
    genotypes = draw_genotypes(jax.random.fold_in(key_of[3], 71), 0)
    probes = gaussian(key_of[1], (NTOT, B), 1.0, 6.0, ((0, 32),))
    missing_codes = with_ends(jax.random.randint(key_of[2], (NTOT,), 0, 2 * NBLK), jax.random.fold_in(key_of[2], 1), 0, (2 * NBLK) - 1).astype(jnp.int32)
    return dict(genotypes=genotypes, probes=probes, missing_codes=missing_codes)


def standardize(geno, codes, mean, inv_sd):
    snp_block = (jnp.arange(M) // BLOCK_SNPS).astype(jnp.int32)
    observed = (snp_block[None, :] != codes[:, None]).astype(jnp.float32)
    return ((geno.astype(jnp.float32) - mean[None, :]) * inv_sd[None, :] * observed).astype(jnp.bfloat16)

def reference(genotypes, probes, missing_codes):
    pieces = N_ROWS
    rows_block = NTOT // pieces
    geno_all = genotypes.reshape(pieces, rows_block, M)
    probe_all = probes.reshape(pieces, rows_block, B)
    code_all = missing_codes.reshape(pieces, rows_block)
    snp_block = (jnp.arange(M) // BLOCK_SNPS).astype(jnp.int32)

    def moment_step(accum, item):
        geno, codes = item
        observed = (snp_block[None, :] != codes[:, None]).astype(jnp.float32)
        dosage = geno.astype(jnp.float32) * observed
        part = jnp.stack([lax.optimization_barrier(jnp.sum(observed, 0)), lax.optimization_barrier(jnp.sum(dosage, 0)), lax.optimization_barrier(jnp.sum(dosage * dosage, 0))])
        return (accum + part, None)
    moments, _ = lax.scan(moment_step, jnp.zeros((3, M), jnp.float32), (geno_all, code_all))
    counted = jnp.maximum(moments[0], 1.0)
    mean = moments[1] / counted
    inv_sd = 1.0 / jnp.sqrt(moments[2] / counted - mean * mean + 1e-05)

    def project_step(accum, item):
        geno, codes, probe = item
        standard = standardize(geno, codes, mean, inv_sd)
        part = jnp.einsum('rs,rb->sb', standard.astype(jnp.float32), probe.astype(jnp.float32), precision=lax.Precision.HIGHEST)
        return (accum + part, None)
    projection, _ = lax.scan(project_step, jnp.zeros((M, B), jnp.float32), (geno_all, code_all, probe_all))
    projection = (projection / math.sqrt(NTOT)).astype(jnp.bfloat16)

    def image_step(accum, item):
        geno, codes = item
        standard = standardize(geno, codes, mean, inv_sd)
        image = (jnp.dot(standard.astype(jnp.float32), projection.astype(jnp.float32), preferred_element_type=jnp.float32) / math.sqrt(M)).astype(jnp.bfloat16)
        wide = image.astype(jnp.float32)
        gram = jnp.einsum('rb,rc->bc', wide, wide, precision=lax.Precision.HIGHEST)
        cross = jnp.einsum('rs,rb->sb', standard.astype(jnp.float32), wide, precision=lax.Precision.HIGHEST)
        return ((accum[0] + gram, accum[1] + cross), image)
    start = (jnp.zeros((B, B), jnp.float32), jnp.zeros((M, B), jnp.float32))
    (gram, cross), images = lax.scan(image_step, start, (geno_all, code_all))
    images = images.reshape(NTOT, B)
    lower = jnp.linalg.cholesky(gram)
    basis = jax.scipy.linalg.solve_triangular(lower, images.astype(jnp.float32).T, lower=True).T * math.sqrt(NTOT)
    scores = jax.scipy.linalg.solve_triangular(lower, cross.T, lower=True).T * math.sqrt(M / NTOT)
    return (basis.astype(jnp.bfloat16), scores.astype(jnp.bfloat16))
```

```python
import functools
import math

import jax
import jax.numpy as jnp
from jax import lax
from jax.experimental import pallas as pl
from jax.experimental.pallas import tpu as pltpu
from jax.sharding import PartitionSpec as P

MESH = pl.DeviceIdType.MESH
BLOCK_SNPS = 128
LANES = 128


def radices(n):
    bits = n.bit_length() - 1
    if n != 1 << bits:
        return [n]
    return [2] * (bits % 2) + [4] * (bits // 2)


def stage_list(sizes):
    stages = []
    for axis in ("cols", "rows"):
        stride = 1
        for radix in radices(sizes[axis]):
            stages.append((axis, stride, radix))
            stride *= radix
    return stages


class Plan:
    def __init__(self, rows, stages, scatter):
        self.rows, self.stages = rows, stages
        self.current, self.split = [rows], []
        for number, (_, _, radix) in enumerate(stages):
            now = self.current[-1]
            split = number in scatter and now % (8 * radix) == 0
            self.split.append(split)
            self.current.append(now // radix if split else now)
        self.copies = 2 * sum(radix - 1 for _, _, radix in stages)
        self.scratch = (
            [pltpu.VMEM((rows, LANES), jnp.float32)] * 2
            + [pltpu.VMEM((r, LANES), jnp.float32) for r in self.current[1:-1]]
            + [
                pltpu.VMEM((radix, r, LANES), jnp.float32)
                for (_, _, radix), r in zip(stages, self.current[1:])
            ]
            + [pltpu.SemaphoreType.DMA((self.copies,)), pltpu.SemaphoreType.DMA((self.copies,))]
        )


class Stream:
    def __init__(self, plan, refs):
        self.plan = plan
        n = len(plan.stages)
        self.source, self.full = refs[0], refs[1]
        self.parts = [refs[0], *refs[2 : n + 1]]
        self.landing = refs[n + 1 : 2 * n + 1]
        self.send_sem, self.recv_sem = refs[2 * n + 1], refs[2 * n + 2]
        self.pending, self.flight, self.used = [], {}, 0
        self.offsets = [0]
        for number, (axis, stride, radix) in enumerate(plan.stages):
            offset = self.offsets[-1]
            if plan.split[number]:
                offset = offset + self.digit(number) * plan.current[number + 1]
            self.offsets.append(offset)

    def digit(self, number):
        axis, stride, radix = self.plan.stages[number]
        return lax.rem(lax.axis_index(axis) // stride, radix)

    def peer(self, number, step):
        axis, stride, radix = self.plan.stages[number]
        digit = self.digit(number)
        other = lax.rem(digit + step, radix)
        return other, {axis: lax.axis_index(axis) + (other - digit) * stride}

    def start(self, key, source, target, device):
        copy = pltpu.make_async_remote_copy(
            src_ref=source,
            dst_ref=target,
            send_sem=self.send_sem.at[self.used],
            recv_sem=self.recv_sem.at[self.used],
            device_id=device,
            device_id_type=MESH,
        )
        self.used += 1
        copy.start()
        self.pending.append(copy)
        self.flight.setdefault(key, []).append(copy)

    def arrive(self, key):
        for copy in self.flight.pop(key):
            copy.wait_recv()

    def send(self, number):
        rows = self.plan.current[number + 1]
        here = self.parts[number]
        for step in range(1, self.plan.stages[number][2]):
            other, device = self.peer(number, step)
            if self.plan.split[number]:
                source = here.at[pl.ds(pl.multiple_of(other * rows, 8), rows)]
            else:
                source = here
            self.start(("out", number), source, self.landing[number].at[self.digit(number)], device)

    def receive(self, number):
        plan = self.plan
        rows, radix = plan.current[number + 1], plan.stages[number][2]
        here, landing, digit = self.parts[number], self.landing[number], self.digit(number)
        if plan.split[number]:
            own = here[pl.ds(pl.multiple_of(digit * rows, 8), rows)]
        else:
            own = here[...]
        landing[digit] = own
        self.arrive(("out", number))
        total = landing[0]
        for other in range(1, radix):
            total = total + landing[other]
        if number + 1 < len(plan.stages):
            self.parts[number + 1][...] = total
        else:
            self.full[pl.ds(pl.multiple_of(self.offsets[-1], 8), rows)] = total

    def spread(self, number):
        if not self.plan.split[number]:
            return
        rows = self.plan.current[number + 1]
        block = self.full.at[pl.ds(pl.multiple_of(self.offsets[number + 1], 8), rows)]
        for step in range(1, self.plan.stages[number][2]):
            _, device = self.peer(number, step)
            self.start(("back", number), block, block, device)

    def gather(self, number):
        if self.plan.split[number]:
            self.arrive(("back", number))

    def finish(self):
        for copy in self.pending:
            copy.wait_send()


def factor(state, columns):
    size = BLOCK_SNPS
    row_at = lax.broadcasted_iota(jnp.int32, (size, size), 0)
    lane_at = lax.broadcasted_iota(jnp.int32, (size, size), 1)

    def step(j, pair):
        left, right = pair
        here = row_at == j
        row = jnp.sum(jnp.where(here, left, 0.0), axis=0, keepdims=True)
        column = jnp.sum(jnp.where(lane_at == j, left, 0.0), axis=1, keepdims=True)
        right_row = jnp.sum(jnp.where(here, right, 0.0), axis=0, keepdims=True)
        pivot = jnp.sum(jnp.where(lane_at[:1] == j, row, 0.0), axis=1, keepdims=True)
        scale = 1.0 / jnp.sqrt(pivot)
        column = jnp.where(row_at > j, column * scale, 0.0)
        left = left - column * (row * scale)
        right_row = right_row * scale
        right = jnp.where(here, right_row, right - column * right_row)
        return left, right

    return lax.fori_loop(*columns, step, state)


def body(sizes, plans, n_inputs, *refs):
    geno_hbm, probes_ref, codes_ref, basis_ref, scores_ref = refs[:5]
    geno, projection, load_sem = refs[5:8]
    rest = refs[8:]
    streams = []
    for plan in plans:
        streams.append(Stream(plan, rest[: len(plan.scratch)]))
        rest = rest[len(plan.scratch) :]
    first, small, second, square_sums = streams
    rows, snps = geno.shape
    blocks = snps // BLOCK_SNPS
    total_rows = rows * sizes["rows"] * sizes["cols"]
    stages = plans[0].stages
    count = len(stages)

    loads = []
    for b in range(blocks):
        cut = pl.ds(b * BLOCK_SNPS, BLOCK_SNPS)
        load = pltpu.make_async_copy(geno_hbm.at[:, cut], geno.at[:, cut], load_sem.at[b])
        load.start()
        loads.append(load)

    barrier = pltpu.get_barrier_semaphore()
    peers = 0
    for number, (_, _, radix) in enumerate(stages):
        for step in range(1, radix):
            _, device = first.peer(number, step)
            pl.semaphore_signal(barrier, inc=1, device_id=device, device_id_type=MESH)
            peers += 1

    probes = probes_ref[...]
    probes_t = probes.astype(jnp.float32).T.astype(jnp.bfloat16)
    codes = codes_ref[...]
    lane = lax.broadcasted_iota(jnp.int32, (rows, LANES), 1)
    seen = (codes != lane).astype(jnp.float32).astype(jnp.bfloat16)
    contract = (((0,), (0,)), ((), ()))
    small.source[0:blocks] = lax.dot_general(
        seen, probes, contract, preferred_element_type=jnp.float32
    )[:blocks]
    small.source[3 * blocks : 4 * blocks] = lax.dot_general(
        seen, jnp.ones_like(probes), contract, preferred_element_type=jnp.float32
    )[:blocks]
    for b in range(blocks):
        cut = slice(b * BLOCK_SNPS, (b + 1) * BLOCK_SNPS)
        loads[b].wait()
        dosage = jnp.where(codes != b, geno[:, cut].astype(jnp.float32), 0.0)
        small.source[blocks + b : blocks + b + 1] = jnp.sum(dosage, axis=0, keepdims=True)
        small.source[2 * blocks + b : 2 * blocks + b + 1] = jnp.sum(
            dosage * dosage, axis=0, keepdims=True
        )
        first.source[cut] = jnp.dot(
            probes_t, dosage.astype(jnp.bfloat16), preferred_element_type=jnp.float32
        )
    pl.semaphore_wait(barrier, peers)

    for number in range(count):
        small.send(number)
        first.send(number)
        small.receive(number)
        first.receive(number)
    for number in reversed(range(count)):
        small.spread(number)
    first.spread(count - 1)
    for number in reversed(range(count)):
        small.gather(number)
    moments = small.full
    counted = jnp.maximum(moments[3 * blocks : 4 * blocks], 1.0)
    mean = moments[blocks : 2 * blocks] / counted
    inv_sd = 1.0 / jnp.sqrt(moments[2 * blocks : 3 * blocks] / counted - mean * mean + 1e-05)
    beside = moments[0:blocks].T
    for number in reversed(range(count)):
        first.gather(number)
        if number:
            first.spread(number - 1)
        if number == count - 1:
            for b in range(blocks):
                cut = slice(b * BLOCK_SNPS, (b + 1) * BLOCK_SNPS)
                centred = (geno[:, cut].astype(jnp.float32) - mean[b : b + 1]) * inv_sd[b : b + 1]
                geno[:, cut] = jnp.where(codes != b, centred, 0.0).astype(jnp.bfloat16)
    for b in range(blocks):
        cut = slice(b * BLOCK_SNPS, (b + 1) * BLOCK_SNPS)
        value = inv_sd[b : b + 1] * (first.full[cut] - mean[b : b + 1] * beside[:, b : b + 1])
        projection[:, cut] = (value / math.sqrt(total_rows)).astype(jnp.bfloat16)

    image = lax.dot_general(
        geno[...], projection[...], (((1,), (1,)), ((), ())), preferred_element_type=jnp.float32
    )
    image = (image / math.sqrt(snps)).astype(jnp.bfloat16)
    image_t = image.astype(jnp.float32).T.astype(jnp.bfloat16)
    square_sums.source[...] = jnp.dot(image_t, image, preferred_element_type=jnp.float32)
    square_sums.send(0)
    for b in range(blocks):
        cut = slice(b * BLOCK_SNPS, (b + 1) * BLOCK_SNPS)
        second.source[cut] = jnp.dot(image_t, geno[:, cut], preferred_element_type=jnp.float32)
    for number in range(count):
        if number:
            square_sums.send(number)
        second.send(number)
        square_sums.receive(number)
        second.receive(number)
    second.spread(count - 1)
    for number in reversed(range(count)):
        square_sums.spread(number)
        square_sums.gather(number)
    eye = (
        lax.broadcasted_iota(jnp.int32, (LANES, LANES), 0)
        == lax.broadcasted_iota(jnp.int32, (LANES, LANES), 1)
    ).astype(jnp.float32)
    state = (square_sums.full[...], eye)
    for number in reversed(range(count)):
        done = count - 1 - number
        state = factor(state, (LANES * done // count, LANES * (done + 1) // count))
        second.gather(number)
        if number:
            second.spread(number - 1)
    inverse = state[1]
    basis = lax.dot_general(
        image.astype(jnp.float32),
        inverse,
        (((1,), (1,)), ((), ())),
        preferred_element_type=jnp.float32,
        precision=lax.Precision.HIGHEST,
    )
    basis_ref[...] = (basis * math.sqrt(total_rows)).astype(jnp.bfloat16)
    for b in range(blocks):
        cut = slice(b * BLOCK_SNPS, (b + 1) * BLOCK_SNPS)
        score = jnp.dot(
            inverse,
            second.full[cut],
            preferred_element_type=jnp.float32,
            precision=lax.Precision.HIGHEST,
        )
        scores_ref[cut] = (score.T * math.sqrt(snps / total_rows)).astype(jnp.bfloat16)
    for stream in streams:
        stream.finish()


def per_device(sizes, genotypes, probes, missing_codes):
    rows, snps = genotypes.shape
    stages = stage_list(sizes)
    everything = range(len(stages))
    plans = [
        Plan(snps, stages, everything),
        Plan(4 * snps // BLOCK_SNPS, stages, (0,)),
        Plan(snps, stages, everything),
        Plan(probes.shape[1], stages, (0,)),
    ]
    scratch = [
        pltpu.VMEM((rows, snps), jnp.bfloat16),
        pltpu.VMEM((LANES, snps), jnp.bfloat16),
        pltpu.SemaphoreType.DMA((snps // BLOCK_SNPS,)),
    ]
    for plan in plans:
        scratch += plan.scratch
    vmem = pl.BlockSpec(memory_space=pltpu.VMEM)
    return pl.pallas_call(
        functools.partial(body, sizes, plans, 3),
        out_shape=(
            jax.ShapeDtypeStruct((rows, LANES), jnp.bfloat16),
            jax.ShapeDtypeStruct((snps, LANES), jnp.bfloat16),
        ),
        in_specs=[pl.BlockSpec(memory_space=pl.ANY), vmem, vmem],
        out_specs=(vmem, vmem),
        scratch_shapes=scratch,
        compiler_params=pltpu.CompilerParams(
            collective_id=0, has_side_effects=True, vmem_limit_bytes=48 * 1024 * 1024
        ),
    )(genotypes, probes, missing_codes[:, None])


def solution(mesh):
    return jax.shard_map(
        functools.partial(per_device, dict(mesh.shape)),
        mesh=mesh,
        in_specs=(P(("rows", "cols"), None), P(("rows", "cols"), None), P(("rows", "cols"))),
        out_specs=(P(("rows", "cols"), None), P()),
        check_vma=False,
    )
```

```python
import functools
import math

import jax
import jax.numpy as jnp
from jax import lax
from jax.experimental import pallas as pl
from jax.experimental.pallas import tpu as pltpu
from jax.sharding import PartitionSpec as P

MESH = pl.DeviceIdType.MESH
BLOCK_SNPS = 128
LANES = 128


def radices(n):
    bits = n.bit_length() - 1
    if n != 1 << bits:
        return [n]
    return [2] * (bits % 2) + [4] * (bits // 2)


def stage_list(sizes):
    stages = []
    for axis in ("cols", "rows"):
        stride = 1
        for radix in radices(sizes[axis]):
            stages.append((axis, stride, radix))
            stride *= radix
    return stages


class Plan:
    def __init__(self, rows, stages, scatter):
        self.rows, self.stages = rows, stages
        self.current, self.split = [rows], []
        for number, (_, _, radix) in enumerate(stages):
            now = self.current[-1]
            split = number in scatter and now % (8 * radix) == 0
            self.split.append(split)
            self.current.append(now // radix if split else now)
        self.copies = 2 * sum(radix - 1 for _, _, radix in stages)
        self.scratch = (
            [pltpu.VMEM((rows, LANES), jnp.float32)] * 2
            + [pltpu.VMEM((r, LANES), jnp.float32) for r in self.current[1:-1]]
            + [
                pltpu.VMEM((radix, r, LANES), jnp.float32)
                for (_, _, radix), r in zip(stages, self.current[1:])
            ]
            + [pltpu.SemaphoreType.DMA((self.copies,)), pltpu.SemaphoreType.DMA((self.copies,))]
        )


class Stream:
    def __init__(self, plan, refs):
        self.plan = plan
        n = len(plan.stages)
        self.source, self.full = refs[0], refs[1]
        self.parts = [refs[0], *refs[2 : n + 1]]
        self.landing = refs[n + 1 : 2 * n + 1]
        self.send_sem, self.recv_sem = refs[2 * n + 1], refs[2 * n + 2]
        self.pending, self.flight, self.used = [], {}, 0
        self.offsets = [0]
        for number, (axis, stride, radix) in enumerate(plan.stages):
            offset = self.offsets[-1]
            if plan.split[number]:
                offset = offset + self.digit(number) * plan.current[number + 1]
            self.offsets.append(offset)

    def digit(self, number):
        axis, stride, radix = self.plan.stages[number]
        return lax.rem(lax.axis_index(axis) // stride, radix)

    def peer(self, number, step):
        axis, stride, radix = self.plan.stages[number]
        digit = self.digit(number)
        other = lax.rem(digit + step, radix)
        return other, {axis: lax.axis_index(axis) + (other - digit) * stride}

    def start(self, key, source, target, device):
        copy = pltpu.make_async_remote_copy(
            src_ref=source,
            dst_ref=target,
            send_sem=self.send_sem.at[self.used],
            recv_sem=self.recv_sem.at[self.used],
            device_id=device,
            device_id_type=MESH,
        )
        self.used += 1
        copy.start()
        self.pending.append(copy)
        self.flight.setdefault(key, []).append(copy)

    def arrive(self, key):
        for copy in self.flight.pop(key):
            copy.wait_recv()

    def send(self, number):
        rows = self.plan.current[number + 1]
        here = self.parts[number]
        for step in range(1, self.plan.stages[number][2]):
            other, device = self.peer(number, step)
            if self.plan.split[number]:
                source = here.at[pl.ds(pl.multiple_of(other * rows, 8), rows)]
            else:
                source = here
            self.start(("out", number), source, self.landing[number].at[self.digit(number)], device)

    def receive(self, number):
        plan = self.plan
        rows, radix = plan.current[number + 1], plan.stages[number][2]
        here, landing, digit = self.parts[number], self.landing[number], self.digit(number)
        if plan.split[number]:
            own = here[pl.ds(pl.multiple_of(digit * rows, 8), rows)]
        else:
            own = here[...]
        landing[digit] = own
        self.arrive(("out", number))
        total = landing[0]
        for other in range(1, radix):
            total = total + landing[other]
        if number + 1 < len(plan.stages):
            self.parts[number + 1][...] = total
        else:
            self.full[pl.ds(pl.multiple_of(self.offsets[-1], 8), rows)] = total

    def spread(self, number):
        if not self.plan.split[number]:
            return
        rows = self.plan.current[number + 1]
        block = self.full.at[pl.ds(pl.multiple_of(self.offsets[number + 1], 8), rows)]
        for step in range(1, self.plan.stages[number][2]):
            _, device = self.peer(number, step)
            self.start(("back", number), block, block, device)

    def gather(self, number):
        if self.plan.split[number]:
            self.arrive(("back", number))

    def finish(self):
        for copy in self.pending:
            copy.wait_send()


def factor(state, columns):
    size = BLOCK_SNPS
    row_at = lax.broadcasted_iota(jnp.int32, (size, size), 0)
    lane_at = lax.broadcasted_iota(jnp.int32, (size, size), 1)

    def step(j, pair):
        left, right = pair
        here = row_at == j
        row = jnp.sum(jnp.where(here, left, 0.0), axis=0, keepdims=True)
        column = jnp.sum(jnp.where(lane_at == j, left, 0.0), axis=1, keepdims=True)
        right_row = jnp.sum(jnp.where(here, right, 0.0), axis=0, keepdims=True)
        pivot = jnp.sum(jnp.where(lane_at[:1] == j, row, 0.0), axis=1, keepdims=True)
        scale = 1.0 / jnp.sqrt(pivot)
        column = jnp.where(row_at > j, column * scale, 0.0)
        left = left - column * (row * scale)
        right_row = right_row * scale
        right = jnp.where(here, right_row, right - column * right_row)
        return left, right

    return lax.fori_loop(*columns, step, state)


def exchange(count, little, pair):
    for number in range(count):
        little.receive(number)
        if number + 1 < count:
            little.send(number + 1)
        for stream in pair:
            stream.receive(number)
            if number + 1 < count:
                stream.send(number + 1)
            else:
                stream.spread(number)


def body(sizes, plans, n_inputs, *refs):
    geno_hbm, probes_ref, codes_ref, basis_ref, scores_ref = refs[:5]
    geno, projection, load_sem = refs[5:8]
    rest = refs[8:]
    streams = []
    for plan in plans:
        streams.append(Stream(plan, rest[: len(plan.scratch)]))
        rest = rest[len(plan.scratch) :]
    firsts, seconds, (small, square_sums) = streams[0:2], streams[2:4], streams[4:6]
    rows, snps = geno.shape
    blocks = snps // BLOCK_SNPS
    half = blocks // 2

    def place(b):
        start = b % half * BLOCK_SNPS
        return b // half, slice(start, start + BLOCK_SNPS)

    total_rows = rows * sizes["rows"] * sizes["cols"]
    stages = plans[0].stages
    count = len(stages)

    loads = []
    for b in range(blocks):
        cut = pl.ds(b * BLOCK_SNPS, BLOCK_SNPS)
        load = pltpu.make_async_copy(geno_hbm.at[:, cut], geno.at[:, cut], load_sem.at[b])
        load.start()
        loads.append(load)

    barrier = pltpu.get_barrier_semaphore()
    peers = 0
    for number, (_, _, radix) in enumerate(stages):
        for step in range(1, radix):
            _, device = firsts[0].peer(number, step)
            pl.semaphore_signal(barrier, inc=1, device_id=device, device_id_type=MESH)
            peers += 1

    probes = probes_ref[...]
    probes_t = probes.astype(jnp.float32).T.astype(jnp.bfloat16)
    codes = codes_ref[...]
    lane = lax.broadcasted_iota(jnp.int32, (rows, LANES), 1)
    seen = (codes != lane).astype(jnp.float32).astype(jnp.bfloat16)
    contract = (((0,), (0,)), ((), ()))
    small.source[0:blocks] = lax.dot_general(
        seen, probes, contract, preferred_element_type=jnp.float32
    )[:blocks]
    small.source[3 * blocks : 4 * blocks] = lax.dot_general(
        seen, jnp.ones_like(probes), contract, preferred_element_type=jnp.float32
    )[:blocks]
    for b in range(blocks):
        cut = slice(b * BLOCK_SNPS, (b + 1) * BLOCK_SNPS)
        loads[b].wait()
        dosage = jnp.where(codes != b, geno[:, cut].astype(jnp.float32), 0.0)
        small.source[blocks + b : blocks + b + 1] = jnp.sum(dosage, axis=0, keepdims=True)
        small.source[2 * blocks + b : 2 * blocks + b + 1] = jnp.sum(
            dosage * dosage, axis=0, keepdims=True
        )
        which, spot = place(b)
        firsts[which].source[spot] = jnp.dot(
            probes_t, dosage.astype(jnp.bfloat16), preferred_element_type=jnp.float32
        )
        if b == half - 1:
            pl.semaphore_wait(barrier, peers)
            firsts[0].send(0)
    small.send(0)
    firsts[1].send(0)
    exchange(count, small, firsts)
    for number in reversed(range(count)):
        small.spread(number)
    for number in reversed(range(count)):
        small.gather(number)
    moments = small.full
    counted = jnp.maximum(moments[3 * blocks : 4 * blocks], 1.0)
    mean = moments[blocks : 2 * blocks] / counted
    inv_sd = 1.0 / jnp.sqrt(moments[2 * blocks : 3 * blocks] / counted - mean * mean + 1e-05)
    beside = moments[0:blocks].T
    for number in reversed(range(count)):
        turn = count - 1 - number
        for b in range(half * turn, half * (turn + 1) if turn < 2 else half * turn):
            cut = slice(b * BLOCK_SNPS, (b + 1) * BLOCK_SNPS)
            centred = (geno[:, cut].astype(jnp.float32) - mean[b : b + 1]) * inv_sd[b : b + 1]
            geno[:, cut] = jnp.where(codes != b, centred, 0.0).astype(jnp.bfloat16)
        for stream in firsts:
            stream.gather(number)
            if number:
                stream.spread(number - 1)
    for b in range(blocks):
        cut = slice(b * BLOCK_SNPS, (b + 1) * BLOCK_SNPS)
        which, spot = place(b)
        value = inv_sd[b : b + 1] * (firsts[which].full[spot] - mean[b : b + 1] * beside[:, b : b + 1])
        projection[:, cut] = (value / math.sqrt(total_rows)).astype(jnp.bfloat16)

    image = lax.dot_general(
        geno[...], projection[...], (((1,), (1,)), ((), ())), preferred_element_type=jnp.float32
    )
    image = (image / math.sqrt(snps)).astype(jnp.bfloat16)
    image_t = image.astype(jnp.float32).T.astype(jnp.bfloat16)
    square_sums.source[...] = jnp.dot(image_t, image, preferred_element_type=jnp.float32)
    square_sums.send(0)
    for b in range(blocks):
        cut = slice(b * BLOCK_SNPS, (b + 1) * BLOCK_SNPS)
        which, spot = place(b)
        seconds[which].source[spot] = jnp.dot(
            image_t, geno[:, cut], preferred_element_type=jnp.float32
        )
        if b % half == half - 1:
            seconds[which].send(0)
    exchange(count, square_sums, seconds)
    for number in reversed(range(count)):
        square_sums.spread(number)
        square_sums.gather(number)
    eye = (
        lax.broadcasted_iota(jnp.int32, (LANES, LANES), 0)
        == lax.broadcasted_iota(jnp.int32, (LANES, LANES), 1)
    ).astype(jnp.float32)
    state = (square_sums.full[...], eye)
    for number in reversed(range(count)):
        done = count - 1 - number
        state = factor(state, (LANES * done // count, LANES * (done + 1) // count))
        for stream in seconds:
            stream.gather(number)
            if number:
                stream.spread(number - 1)
    inverse = state[1]
    basis = lax.dot_general(
        image.astype(jnp.float32),
        inverse,
        (((1,), (1,)), ((), ())),
        preferred_element_type=jnp.float32,
        precision=lax.Precision.HIGHEST,
    )
    basis_ref[...] = (basis * math.sqrt(total_rows)).astype(jnp.bfloat16)
    for b in range(blocks):
        cut = slice(b * BLOCK_SNPS, (b + 1) * BLOCK_SNPS)
        score = jnp.dot(
            inverse,
            seconds[place(b)[0]].full[place(b)[1]],
            preferred_element_type=jnp.float32,
            precision=lax.Precision.HIGHEST,
        )
        scores_ref[cut] = (score.T * math.sqrt(snps / total_rows)).astype(jnp.bfloat16)
    for stream in streams:
        stream.finish()


def per_device(sizes, genotypes, probes, missing_codes):
    rows, snps = genotypes.shape
    stages = stage_list(sizes)
    everything = range(len(stages))
    turned = stages[:1] + stages[:0:-1]
    plans = [
        Plan(snps // 2, stages, everything),
        Plan(snps // 2, turned, everything),
        Plan(snps // 2, stages, everything),
        Plan(snps // 2, turned, everything),
        Plan(4 * snps // BLOCK_SNPS, stages, (0,)),
        Plan(probes.shape[1], stages, (0,)),
    ]
    scratch = [
        pltpu.VMEM((rows, snps), jnp.bfloat16),
        pltpu.VMEM((LANES, snps), jnp.bfloat16),
        pltpu.SemaphoreType.DMA((snps // BLOCK_SNPS,)),
    ]
    for plan in plans:
        scratch += plan.scratch
    vmem = pl.BlockSpec(memory_space=pltpu.VMEM)
    return pl.pallas_call(
        functools.partial(body, sizes, plans, 3),
        out_shape=(
            jax.ShapeDtypeStruct((rows, LANES), jnp.bfloat16),
            jax.ShapeDtypeStruct((snps, LANES), jnp.bfloat16),
        ),
        in_specs=[pl.BlockSpec(memory_space=pl.ANY), vmem, vmem],
        out_specs=(vmem, vmem),
        scratch_shapes=scratch,
        compiler_params=pltpu.CompilerParams(
            collective_id=0, has_side_effects=True, vmem_limit_bytes=48 * 1024 * 1024
        ),
    )(genotypes, probes, missing_codes[:, None])


def solution(mesh):
    return jax.shard_map(
        functools.partial(per_device, dict(mesh.shape)),
        mesh=mesh,
        in_specs=(P(("rows", "cols"), None), P(("rows", "cols"), None), P(("rows", "cols"))),
        out_specs=(P(("rows", "cols"), None), P()),
        check_vma=False,
    )
```
